256 devices in a mesh: dom: 8 (over x, core), mem: 32 (over z, y).
Axes of the slice: x: 4, y: 4, z: 8, core: 2. Of those that a mesh axis runs over, the one named last changes fastest.
Arguments:
- state: float32 [1024, 262144], P('mem', 'dom'), may hold values from -14 to 14, as said below
- obs_ensemble: float32 [1024, 4096], P('mem', 'dom'), may hold values from -14 to 14, as said below
- innovations: float32 [1024, 4096], P('mem', 'dom'), may hold values from -6 to 6
- obs_coords: float32 [2, 4096], P(None, 'dom'), may hold values from 0 to 8, as said below
- tile_list: int32 [8, 32, 2, 48], P('dom', 'mem'), may hold values from 0 to 11, as said below
- tile_counts: int32 [8, 32], P('dom', 'mem'), may hold values from 24 to 48, as said below
Outputs:
- analysis: float32 [1024, 262144], P(None, ('dom', 'mem'))
The draws below stay inside these ranges and needn't reach their ends.
Inputs may be any that keep to these rules, and one draw needn't show every extreme that they name: `state`: forecast values of each gridpoint: an offset plus a spread of its own times a bounded noise. `obs_ensemble`: Observation-space values of each observation: an offset plus a spread of its own times a bounded noise. `obs_coords`: the observations of domain d have a first coordinate within [d, d + 1) and a second within [0, 1). `tile_list`: slots k * 6 to (k + 1) * 6 - 1 name point block k (of 8) and 6 distinct observation blocks of the window of 12 blocks: the left neighbour domain's, the own domain's, the right neighbour domain's, domains on a cycle. `tile_counts`: slots below the count are live. Some group has all 48 live, some other group half of them.
All inputs are finite; a program needn't handle non-finite values.
Results may differ from the reference program's by a relative error of at most 0.0002.
Values sent between devices are 32-bit elements; how exact they have to be, the bound alone decides.
A program may use at most 192 MiB of HBM per device.

```python
import jax
import jax.numpy as jnp
from jax import lax

M = 1024
BLK = 128
PTS_DEV = 1024
OBS_DOM = 512
TPB = 6
DOMAINS = 8
GROUPS = 32
PTS_DOM = 32768
PTS = 262144
OBS = 4096
TILES = 48


def draw_spread(key, rows, columns):
    key_offset, key_scale, key_noise = jax.random.split(key, 3)
    offset = jax.random.uniform(key_offset, (1, columns), jnp.float32, -2.0, 2.0)
    scale = jnp.exp(jax.random.uniform(key_scale, (1, columns), jnp.float32, jnp.log(0.3), jnp.log(3.0)))
    noise = jax.random.truncated_normal(key_noise, -4.0, 4.0, (rows, columns), jnp.float32)
    return offset + scale * noise


def draw_state(key, part):
    return draw_spread(jax.random.fold_in(key, 11), M, PTS)


def draw_obs_ensemble(key, part):
    return draw_spread(jax.random.fold_in(key, 23), M, OBS)


def draw_obs_coords(key, part):
    key_x, key_y = jax.random.split(jax.random.fold_in(key, 37))
    domain = (jnp.arange(OBS) // OBS_DOM).astype(jnp.float32)
    along = jax.random.uniform(key_x, (OBS,), jnp.float32, 0.0, 0.999)
    across = jax.random.uniform(key_y, (OBS,), jnp.float32, 0.0, 1.0)
    return jnp.stack([domain + along, across], axis=0)


def block_order(subkey):
    return jax.random.permutation(subkey, 3 * (OBS_DOM // BLK))[:TPB]


def draw_tile_list(key, part):
    nblocks = PTS_DEV // BLK
    subkeys = jax.random.split(jax.random.fold_in(key, 41), DOMAINS * GROUPS * nblocks)
    orders = jax.vmap(block_order)(subkeys)
    obs_part = orders.reshape(DOMAINS, GROUPS, nblocks * TPB).astype(jnp.int32)
    point_part = jnp.broadcast_to((jnp.arange(nblocks * TPB, dtype=jnp.int32) // TPB)[None, None, :], (DOMAINS, GROUPS, nblocks * TPB))
    return jnp.stack([point_part, obs_part], axis=2).astype(jnp.int32)


def draw_tile_counts(key, part):
    key_count, key_pick = jax.random.split(jax.random.fold_in(key, 53))
    total = DOMAINS * GROUPS
    counts = jax.random.randint(key_count, (total,), TILES // 2, TILES + 1)
    chosen = jax.random.randint(key_pick, (), 0, total)
    counts = counts.at[chosen].set(TILES)
    counts = counts.at[(chosen + 1) % total].set(TILES // 2)
    return counts.reshape(DOMAINS, GROUPS).astype(jnp.int32)


def shard_levels(own_key, extent, cuts, least, top_value):
    factor_of = 1.0
    for dim, parts in cuts:
        heights = jax.random.uniform(jax.random.fold_in(jax.random.fold_in(own_key, 6), dim), (parts,), jnp.float32, least / len(cuts), top_value / len(cuts))
        factor_of = factor_of * jnp.repeat(jnp.exp(heights), extent[dim] // parts).reshape((-1,) + (1,) * (len(extent) - 1 - dim))
    return factor_of


def centred(key, extent, scale, reach, cuts=(), kind=jnp.bfloat16):
    array = jax.random.normal(key, extent, jnp.float32) * scale
    if len(cuts) > 0:
        array = shard_levels(key, extent, cuts, -0.22, 0.18) * array
    return jnp.clip(array, min=-reach, max=reach).astype(kind)


def setup_inputs(seed: int = 0) -> dict:
    key_of = jax.random.split(jax.random.key(seed), 7)
    return {
        "state": draw_state(jax.random.fold_in(key_of[6], 71), 0),
        "obs_ensemble": draw_obs_ensemble(jax.random.fold_in(key_of[6], 71), 0),
        "innovations": centred(key_of[2], (M, OBS), 1.0, 6.0, ((0, 32), (1, 8)), jnp.float32),
        "obs_coords": draw_obs_coords(jax.random.fold_in(key_of[6], 71), 0),
        "tile_list": draw_tile_list(jax.random.fold_in(key_of[6], 71), 0),
        "tile_counts": draw_tile_counts(jax.random.fold_in(key_of[6], 71), 0),
    }


taper_reach = 0.6


def taper_of(point_x, point_y, obs_x, obs_y, cycle_size):
    gap_x = jnp.abs(point_x[:, :, None] - obs_x[:, None, :])
    gap_x = jnp.minimum(gap_x, cycle_size - gap_x)
    gap_y = point_y[:, :, None] - obs_y[:, None, :]
    return jnp.exp(-(gap_x * gap_x + gap_y * gap_y) / (2.0 * taper_reach * taper_reach))


def reference(state, obs_ensemble, innovations, obs_coords, tile_list, tile_counts):
    anomalies = obs_ensemble - jnp.mean(obs_ensemble, axis=0, keepdims=True)
    obs_blocks = OBS_DOM // BLK
    cycle_size = float(DOMAINS)
    row_count = float(PTS_DOM // 32)

    def one_device(device, output):
        device = jnp.asarray(device).astype(jnp.int32)
        domain = device // GROUPS
        group_id = device % GROUPS
        start = (domain * PTS_DOM + group_id * PTS_DEV).astype(jnp.int32)
        live_count = tile_counts[domain, group_id]

        def one_tile(slot_index, change):
            slot_index = jnp.asarray(slot_index).astype(jnp.int32)
            pblock = tile_list[domain, group_id, 0, slot_index]
            oblock = tile_list[domain, group_id, 1, slot_index]
            src_domain = (domain - 1 + oblock // obs_blocks + DOMAINS) % DOMAINS
            column = (src_domain * OBS_DOM + (oblock % obs_blocks) * BLK).astype(jnp.int32)
            offset = (pblock * BLK).astype(jnp.int32)
            x_block = lax.dynamic_slice_in_dim(state, start + offset, BLK, 1)
            y_block = lax.dynamic_slice_in_dim(anomalies, column, BLK, 1)
            w_block = lax.dynamic_slice_in_dim(innovations, column, BLK, 1)
            c_block = lax.dynamic_slice_in_dim(obs_coords, column, BLK, 1)
            covariance = jnp.dot(x_block.T, y_block, precision=lax.Precision.HIGHEST) / (M - 1)
            within = group_id * PTS_DEV + pblock * BLK + jnp.arange(BLK, dtype=jnp.int32)
            point_x = domain.astype(jnp.float32) + ((within % 32).astype(jnp.float32) + 0.5) / 32.0
            point_y = ((within // 32).astype(jnp.float32) + 0.5) / row_count
            taper = taper_of(point_x[None], point_y[None], c_block[0][None], c_block[1][None], cycle_size)[0]
            live_mask = (slot_index < live_count).astype(jnp.float32)
            weights = taper * covariance * live_mask
            increment = jnp.dot(w_block, weights.T, precision=lax.Precision.HIGHEST)
            before = lax.dynamic_slice_in_dim(change, offset, BLK, 1)
            return lax.dynamic_update_slice_in_dim(change, before + increment, offset, 1)

        change = lax.fori_loop(0, TILES, one_tile, jnp.zeros((M, PTS_DEV), jnp.float32))
        updated = lax.dynamic_slice_in_dim(state, start, PTS_DEV, 1) + change
        return lax.dynamic_update_slice_in_dim(output, updated, start, 1)

    return lax.fori_loop(0, DOMAINS * GROUPS, one_device, state)
```

```python
import jax
import jax.numpy as jnp
from jax import lax
from jax.experimental import pallas as pl
from jax.experimental.pallas import tpu as pltpu
from jax.sharding import PartitionSpec as P

taper_reach = 0.6
f32, bf16 = jnp.float32, jnp.bfloat16
ZN, YN = 8, 4
MEM = ZN * YN
DOM = 8
ROWS = 32
M = 1024
OBS = 512
BLK = 128
NB = 8
TPB = 6
PTS = NB * BLK


def halves(v):
    high = v.astype(bf16)
    return high, (v - high.astype(f32)).astype(bf16)


def remote(src, dst, send, recv, device):
    return pltpu.make_async_remote_copy(
        src_ref=src,
        dst_ref=dst,
        send_sem=send,
        recv_sem=recv,
        device_id=device,
        device_id_type=pl.DeviceIdType.MESH,
    )


def kernel(
    tiles, count, state, ens, innov, coords, out,
    xbuf, win, crd, at_hi, at_lo, in_hi, in_lo, cx, cy, obuf,
    obs_local, own_local, crd_send, z_send, y_send, x_send, a_send,
    blk_recv, x_recv, crd_recv, a_recv, out_sem,
):
    d = lax.axis_index("dom")
    me = lax.axis_index("mem")
    z, y = lax.div(me, YN), lax.rem(me, YN)
    right, left = lax.rem(d + 1, DOM), lax.rem(d + DOM - 1, DOM)

    def mem_of(dz, dy):
        return lax.rem(z + dz + ZN, ZN) * YN + lax.rem(y + dy + YN, YN)

    def rows(m):
        return pl.ds(pl.multiple_of(m * ROWS, ROWS), ROWS)

    own_obs = [
        pltpu.make_async_copy(ens, win.at[1, 0, rows(me), :], obs_local.at[0]),
        pltpu.make_async_copy(innov, win.at[1, 1, rows(me), :], obs_local.at[1]),
        pltpu.make_async_copy(coords, crd.at[1], obs_local.at[2]),
    ]
    for c in own_obs:
        c.start()

    def own_state(k):
        cols = pl.ds(pl.multiple_of(me * PTS + k * BLK, BLK), BLK)
        return pltpu.make_async_copy(state.at[:, cols], xbuf.at[k, rows(me), :], own_local.at[k])

    for k in range(NB):
        own_state(k).start()

    barrier = pltpu.get_barrier_semaphore()

    def greet(i, c):
        pl.semaphore_signal(
            barrier, inc=1, device_id=(d, lax.rem(me + i, MEM)), device_id_type=pl.DeviceIdType.MESH
        )
        return c

    for other in (left, right):
        pl.semaphore_signal(
            barrier, inc=1, device_id=(other, me), device_id_type=pl.DeviceIdType.MESH
        )
    lax.fori_loop(1, MEM, greet, 0)
    pl.semaphore_wait(barrier, MEM + 1)
    for c in own_obs:
        c.wait()

    def block(m):
        return win.at[1, :, rows(m), :]

    def half(t, m):
        return win.at[1, t, rows(m), :]

    def push(src, m, dz, dy, send):
        remote(src, src, send, blk_recv.at[m], (d, mem_of(dz, dy))).start()

    def push_z(m, way):
        push(block(m), m, way, 0, z_send)

    def push_y(m):
        push(block(m), m, 0, 1, y_send)
        push(block(m), m, 0, -1, y_send)

    def push_x(m):
        remote(block(m), win.at[2, :, rows(m), :], x_send.at[0], x_recv.at[1], (left, me)).start()
        remote(block(m), win.at[0, :, rows(m), :], x_send.at[1], x_recv.at[0], (right, me)).start()

    def take(m):
        remote(block(m), block(m), z_send, blk_recv.at[m], (d, mem_of(1, 0))).wait_recv()

    def send_state(k):
        def one(i, c):
            j, dy = lax.rem(i, ZN), lax.div(i, ZN)
            h = lax.div(j + 1, 2)
            dz = jnp.where(lax.rem(j, 2) == 1, h, ZN - h)
            to = mem_of(dz, dy)
            cols = pl.ds(pl.multiple_of(to * PTS + k * BLK, BLK), BLK)
            remote(
                state.at[:, cols], xbuf.at[k, rows(me), :], a_send, a_recv.at[k], (d, to)
            ).start()
            return c

        lax.fori_loop(1, MEM, one, 0)

    def column(dz):
        lo, hi = mem_of(dz, -1), mem_of(dz, 1)
        take(lo)
        push(half(0, lo), lo, 0, 1, y_send)
        push_x(lo)
        take(hi)
        push(half(1, hi), hi, 0, -1, y_send)
        push_x(hi)

    push_z(me, 1)
    push_z(me, -1)
    push_y(me)
    coord_copies = [
        remote(coords, crd.at[2], crd_send.at[0], crd_recv.at[1], (left, me)),
        remote(coords, crd.at[0], crd_send.at[1], crd_recv.at[0], (right, me)),
    ]
    for c in coord_copies:
        c.start()
    push_x(me)
    send_state(0)
    for s in range(1, ZN // 2 + 1):
        if s < ZN // 2:
            up, down = mem_of(-s, 0), mem_of(s, 0)
            for m, way, t in ((up, 1, 0), (down, -1, 1)):
                take(m)
                if s < ZN // 2 - 1:
                    push_z(m, way)
                else:
                    push(half(t, m), m, way, 0, z_send)
                push_y(m)
                push_x(m)
        else:
            m = mem_of(s, 0)
            take(m)
            push_y(m)
            push_x(m)
        column(1 - s)
        if s > 1:
            column(s - 1)
        send_state(s)
    column(ZN // 2)
    send_state(5)

    def far(dz, c):
        m = mem_of(dz, 2)
        take(m)
        push_x(m)
        return c

    lax.fori_loop(0, ZN, far, 0)
    send_state(6)
    send_state(7)

    def prepare(slot):
        def one(j, c):
            b = slot * (OBS // BLK) + j
            cols = pl.ds(pl.multiple_of(j * BLK, BLK), BLK)
            v = win[slot, 0, :, cols]
            v = v - jnp.sum(v, axis=0, keepdims=True) * (1.0 / M)
            at_hi[b], at_lo[b] = halves(v.T)
            in_hi[b], in_lo[b] = halves(win[slot, 1, :, cols])
            cx[b] = jnp.broadcast_to(crd[slot, 0:1, cols], (BLK, BLK)).T
            cy[b] = jnp.broadcast_to(crd[slot, 1:2, cols], (BLK, BLK)).T
            return c

        lax.fori_loop(0, OBS // BLK, one, 0)

    prepare(1)
    for c in coord_copies:
        c.wait()
    for slot, n in ((0, 0), (2, 1)):
        pltpu.make_async_copy(win.at[slot], win.at[slot], x_recv.at[n]).wait()
        prepare(slot)

    def put(k):
        cols = pl.ds(pl.multiple_of(k * BLK, BLK), BLK)
        s = lax.rem(k, 2)
        return pltpu.make_async_copy(obuf.at[s], out.at[:, cols], out_sem.at[s])

    def piece(k, c):
        got = xbuf.at[k, pl.ds(0, M - ROWS), :]
        pltpu.make_async_copy(got, got, a_recv.at[k]).wait()
        own_state(k).wait()
        ids = [tiles[1, k * TPB + t] for t in range(TPB)]
        x = xbuf[k]
        xh, xl = halves(x)
        xs = jnp.concatenate([xh, xl], axis=1)
        ah = jnp.concatenate([at_hi[b] for b in ids], axis=0)
        al = jnp.concatenate([at_lo[b] for b in ids], axis=0)
        c1 = jnp.dot(ah, xs, preferred_element_type=f32)
        c2 = jnp.dot(al, xh, preferred_element_type=f32)
        cov = c1[:, :BLK] + (c1[:, BLK:] + c2)
        lane = lax.broadcasted_iota(jnp.int32, (1, BLK), 1)
        px = d.astype(f32) + (lax.rem(lane, 32).astype(f32) + 0.5) / 32.0
        first = me * (PTS // 32) + k * (BLK // 32)
        py = ((first + lax.div(lane, 32)).astype(f32) + 0.5) / float(MEM * PTS // 32)
        w = []
        for t in range(TPB):
            gx = jnp.abs(px - cx[ids[t]])
            gx = jnp.minimum(gx, float(DOM) - gx)
            gy = py - cy[ids[t]]
            taper = jnp.exp(-(gx * gx + gy * gy) / (2.0 * taper_reach * taper_reach))
            alive = jnp.where(k * TPB + t < count[0, 0], 1.0 / (M - 1), 0.0)
            w.append(taper * cov[t * BLK : (t + 1) * BLK] * alive)
        wh, wl = halves(jnp.concatenate(w, axis=0))
        ws = jnp.concatenate([wh, wl], axis=1)
        ih = jnp.concatenate([in_hi[b] for b in ids], axis=1)
        il = jnp.concatenate([in_lo[b] for b in ids], axis=1)
        r1 = jnp.dot(ih, ws, preferred_element_type=f32)
        r2 = jnp.dot(il, wh, preferred_element_type=f32)

        @pl.when(k >= 2)
        def _():
            put(k - 2).wait()

        obuf[lax.rem(k, 2)] = x + (r1[:, :BLK] + (r1[:, BLK:] + r2))
        put(k).start()
        return c

    lax.fori_loop(0, NB, piece, 0)
    put(NB - 2).wait()
    put(NB - 1).wait()

    def drain(ref, sem):
        pltpu.make_async_copy(ref, ref, sem).wait()

    drain(win.at[1, :, pl.ds(0, 7 * ROWS), :], z_send)
    drain(win.at[1, :, pl.ds(0, 24 * ROWS), :], y_send)
    drain(win.at[1], x_send.at[0])
    drain(win.at[1], x_send.at[1])
    drain(state.at[:, pl.ds(0, (MEM - 1) * PTS)], a_send)


def shards(state, obs_ensemble, innovations, obs_coords, tile_list, tile_counts):
    hbm = pl.BlockSpec(memory_space=pl.ANY)
    smem = pl.BlockSpec(memory_space=pltpu.SMEM)
    vmem = pl.BlockSpec(memory_space=pltpu.VMEM)
    dma = pltpu.SemaphoreType.DMA
    return pl.pallas_call(
        kernel,
        out_shape=jax.ShapeDtypeStruct((M, PTS), f32),
        in_specs=[smem, smem, hbm, hbm, hbm, vmem],
        out_specs=hbm,
        scratch_shapes=[
            pltpu.VMEM((NB, M, BLK), f32),
            pltpu.VMEM((3, 2, M, OBS), f32),
            pltpu.VMEM((3, 2, OBS), f32),
            pltpu.VMEM((12, BLK, M), bf16),
            pltpu.VMEM((12, BLK, M), bf16),
            pltpu.VMEM((12, M, BLK), bf16),
            pltpu.VMEM((12, M, BLK), bf16),
            pltpu.VMEM((12, BLK, BLK), f32),
            pltpu.VMEM((12, BLK, BLK), f32),
            pltpu.VMEM((2, M, BLK), f32),
            dma((3,)),
            dma((NB,)),
            dma((2,)),
            dma,
            dma,
            dma((2,)),
            dma,
            dma((MEM,)),
            dma((2,)),
            dma((2,)),
            dma((NB,)),
            dma((2,)),
        ],
        compiler_params=pltpu.CompilerParams(
            collective_id=0, has_side_effects=True, vmem_limit_bytes=60 * 1024 * 1024
        ),
        name="update",
    )(tile_list[0, 0], tile_counts, state, obs_ensemble, innovations, obs_coords)


def solution(mesh):
    return jax.shard_map(
        shards,
        mesh=mesh,
        in_specs=(
            P("mem", "dom"),
            P("mem", "dom"),
            P("mem", "dom"),
            P(None, "dom"),
            P("dom", "mem", None, None),
            P("dom", "mem"),
        ),
        out_specs=P(None, ("dom", "mem")),
        check_vma=False,
    )
```

```python
import jax
import jax.numpy as jnp
from jax import lax
from jax.experimental import pallas as pl
from jax.experimental.pallas import tpu as pltpu
from jax.sharding import PartitionSpec as P

taper_reach = 0.6
f32, bf16 = jnp.float32, jnp.bfloat16
ZN, YN = 8, 4
MEM = ZN * YN
DOM = 8
ROWS = 32
M = 1024
OBS = 512
BLK = 128
NB = 8
TPB = 6
PTS = NB * BLK


def halves(v):
    high = v.astype(bf16)
    return high, (v - high.astype(f32)).astype(bf16)


def remote(src, dst, send, recv, device):
    return pltpu.make_async_remote_copy(
        src_ref=src,
        dst_ref=dst,
        send_sem=send,
        recv_sem=recv,
        device_id=device,
        device_id_type=pl.DeviceIdType.MESH,
    )


def kernel(
    tiles_hbm, count, state, ens, innov, coords, out,
    tiles, xbuf, win, crd, at_hi, at_lo, in_hi, in_lo, cx, cy,
    obs_local, own_local, crd_send, z_send, y_send, x_send, a_send,
    blk_recv, x_recv, crd_recv, a_recv, token,
):
    d = lax.axis_index("dom")
    me = lax.axis_index("mem")
    z, y = lax.div(me, YN), lax.rem(me, YN)
    right, left = lax.rem(d + 1, DOM), lax.rem(d + DOM - 1, DOM)

    def mem_of(dz, dy):
        return lax.rem(z + dz + ZN, ZN) * YN + lax.rem(y + dy + YN, YN)

    def rows(m):
        return pl.ds(pl.multiple_of(m * ROWS, ROWS), ROWS)

    own_obs = [
        pltpu.make_async_copy(ens, win.at[1, 0, rows(me), :], obs_local.at[0]),
        pltpu.make_async_copy(innov, win.at[1, 1, rows(me), :], obs_local.at[1]),
    ]
    small = [
        pltpu.make_async_copy(coords, crd.at[1], obs_local.at[2]),
        pltpu.make_async_copy(tiles_hbm, tiles, obs_local.at[3]),
    ]
    for c in own_obs + small:
        c.start()

    def own_state(k):
        cols = pl.ds(pl.multiple_of(me * PTS + k * BLK, BLK), BLK)
        return pltpu.make_async_copy(state.at[:, cols], xbuf.at[k, rows(me), :], own_local.at[k])

    barrier = pltpu.get_barrier_semaphore()
    around = [(d, mem_of(1, 0)), (d, mem_of(-1, 0)), (d, mem_of(0, 1)), (d, mem_of(0, -1))]

    def signal(sem, device):
        pl.semaphore_signal(sem, inc=1, device_id=device, device_id_type=pl.DeviceIdType.MESH)

    for device in around + [(left, me), (right, me)]:
        signal(barrier, device)
    for c in own_obs:
        c.wait()
    pl.semaphore_wait(barrier, 6)

    def block(m):
        return win.at[1, :, rows(m), :]

    def half(t, m):
        return win.at[1, t, rows(m), :]

    def push(src, m, dz, dy, send):
        remote(src, src, send, blk_recv.at[m], (d, mem_of(dz, dy))).start()

    def push_z(m, way):
        push(block(m), m, way, 0, z_send)

    def push_y(m):
        push(block(m), m, 0, 1, y_send)
        push(block(m), m, 0, -1, y_send)

    def push_x(m):
        remote(block(m), win.at[2, :, rows(m), :], x_send.at[0], x_recv.at[1], (left, me)).start()
        remote(block(m), win.at[0, :, rows(m), :], x_send.at[1], x_recv.at[0], (right, me)).start()

    def take(m):
        remote(block(m), block(m), z_send, blk_recv.at[m], (d, mem_of(1, 0))).wait_recv()

    def send_to(k, to):
        cols = pl.ds(pl.multiple_of(to * PTS + k * BLK, BLK), BLK)
        remote(state.at[:, cols], xbuf.at[k, rows(me), :], a_send, a_recv.at[k], (d, to)).start()

    def send_near(k, c):
        for dz, dy in ((1, 0), (-1, 0), (0, 1), (0, -1)):
            send_to(k, mem_of(dz, dy))
        return c

    def send_state(k):
        def one(i, c):
            wide, mid = i < ZN, i < 3 * ZN - 2
            j = jnp.where(wide, i, jnp.where(mid, lax.div(i - ZN, 2), i - (3 * ZN - 2)))
            dy = jnp.where(wide, 2, jnp.where(mid, 1 + 2 * lax.rem(i, 2), 0))
            h = lax.div(j + 1, 2)
            dz = jnp.where(lax.rem(j, 2) == 1, ZN // 2 - h, ZN // 2 + h)
            send_to(k, mem_of(dz, dy))
            return c

        lax.fori_loop(0, MEM - 5, one, 0)

    def column(dz):
        lo, hi = mem_of(dz, -1), mem_of(dz, 1)
        take(lo)
        push(half(0, lo), lo, 0, 1, y_send)
        push_x(lo)
        take(hi)
        push(half(1, hi), hi, 0, -1, y_send)
        push_x(hi)

    push_z(me, 1)
    push_z(me, -1)
    push_y(me)
    coord_copies = [
        remote(coords, crd.at[2], crd_send.at[0], crd_recv.at[1], (left, me)),
        remote(coords, crd.at[0], crd_send.at[1], crd_recv.at[0], (right, me)),
    ]
    for c in coord_copies:
        c.start()
    lax.fori_loop(0, NB - 1, send_near, 0)
    push_x(me)
    for k in range(NB):
        own_state(k).start()
    for n in range(5):
        side = around[:2] if n < 3 else around[2:]
        for w in range(2):
            signal(token.at[n, w], side[w])
        for w in range(2):
            pl.semaphore_wait(token.at[n, w], 1)
    send_state(0)
    for s in range(1, ZN // 2 + 1):
        if s < ZN // 2:
            up, down = mem_of(-s, 0), mem_of(s, 0)
            for m, way, t in ((up, 1, 0), (down, -1, 1)):
                take(m)
                if s < ZN // 2 - 1:
                    push_z(m, way)
                else:
                    push(half(t, m), m, way, 0, z_send)
                push_y(m)
                push_x(m)
        else:
            m = mem_of(s, 0)
            take(m)
            push_y(m)
            push_x(m)
        column(1 - s)
        if s > 1:
            column(s - 1)
        send_state(s)
    column(ZN // 2)
    send_state(5)

    def far(dz, c):
        m = mem_of(dz, 2)
        take(m)
        push_x(m)
        return c

    lax.fori_loop(0, ZN, far, 0)
    send_state(6)
    send_state(7)
    send_near(NB - 1, 0)

    def prepare(slot):
        def one(j, c):
            b = slot * (OBS // BLK) + j
            cols = pl.ds(pl.multiple_of(j * BLK, BLK), BLK)
            v = win[slot, 0, :, cols]
            v = v - jnp.sum(v, axis=0, keepdims=True) * (1.0 / M)
            at_hi[b], at_lo[b] = halves(v.T)
            in_hi[b], in_lo[b] = halves(win[slot, 1, :, cols])
            cx[b] = jnp.broadcast_to(crd[slot, 0:1, cols], (BLK, BLK)).T
            cy[b] = jnp.broadcast_to(crd[slot, 1:2, cols], (BLK, BLK)).T
            return c

        lax.fori_loop(0, OBS // BLK, one, 0)

    for c in small:
        c.wait()
    prepare(1)
    for c in coord_copies:
        c.wait()
    for slot, n in ((0, 0), (2, 1)):
        pltpu.make_async_copy(win.at[slot], win.at[slot], x_recv.at[n]).wait()
        prepare(slot)

    def piece(k, c):
        got = xbuf.at[k, pl.ds(0, M - ROWS), :]
        pltpu.make_async_copy(got, got, a_recv.at[k]).wait()
        own_state(k).wait()
        ids = [tiles[1, k * TPB + t] for t in range(TPB)]
        x = xbuf[k]
        xh, xl = halves(x)
        xs = jnp.concatenate([xh, xl], axis=1)
        ah = jnp.concatenate([at_hi[b] for b in ids], axis=0)
        al = jnp.concatenate([at_lo[b] for b in ids], axis=0)
        c1 = jnp.dot(ah, xs, preferred_element_type=f32)
        c2 = jnp.dot(al, xh, preferred_element_type=f32)
        cov = c1[:, :BLK] + (c1[:, BLK:] + c2)
        lane = lax.broadcasted_iota(jnp.int32, (1, BLK), 1)
        px = d.astype(f32) + (lax.rem(lane, 32).astype(f32) + 0.5) / 32.0
        first = me * (PTS // 32) + k * (BLK // 32)
        py = ((first + lax.div(lane, 32)).astype(f32) + 0.5) / float(MEM * PTS // 32)
        w = []
        for t in range(TPB):
            gx = jnp.abs(px - cx[ids[t]])
            gx = jnp.minimum(gx, float(DOM) - gx)
            gy = py - cy[ids[t]]
            taper = jnp.exp(-(gx * gx + gy * gy) / (2.0 * taper_reach * taper_reach))
            alive = jnp.where(k * TPB + t < count[0, 0], 1.0 / (M - 1), 0.0)
            w.append(taper * cov[t * BLK : (t + 1) * BLK] * alive)
        wh, wl = halves(jnp.concatenate(w, axis=0))
        ws = jnp.concatenate([wh, wl], axis=1)
        ih = jnp.concatenate([in_hi[b] for b in ids], axis=1)
        il = jnp.concatenate([in_lo[b] for b in ids], axis=1)
        r1 = jnp.dot(ih, ws, preferred_element_type=f32)
        r2 = jnp.dot(il, wh, preferred_element_type=f32)

        cols = pl.ds(pl.multiple_of(k * BLK, BLK), BLK)
        out[:, cols] = x + (r1[:, :BLK] + (r1[:, BLK:] + r2))
        return c

    lax.fori_loop(0, NB, piece, 0)

    def drain(ref, sem):
        pltpu.make_async_copy(ref, ref, sem).wait()

    drain(win.at[1, :, pl.ds(0, 7 * ROWS), :], z_send)
    drain(win.at[1, :, pl.ds(0, 24 * ROWS), :], y_send)
    drain(win.at[1], x_send.at[0])
    drain(win.at[1], x_send.at[1])
    drain(state.at[:, pl.ds(0, (MEM - 1) * PTS)], a_send)


def pinned(a):
    return a if a.size == 1 else pltpu.with_memory_space_constraint(a, pltpu.HBM)


def shards(state, obs_ensemble, innovations, obs_coords, tile_list, tile_counts):
    hbm = pl.BlockSpec(memory_space=pltpu.HBM)
    vmem = pl.BlockSpec(memory_space=pltpu.VMEM)
    dma = pltpu.SemaphoreType.DMA
    return pl.pallas_call(
        kernel,
        out_shape=pltpu.VMEM((M, PTS), f32),
        in_specs=[hbm, pl.BlockSpec(memory_space=pltpu.SMEM), hbm, hbm, hbm, hbm],
        out_specs=vmem,
        scratch_shapes=[
            pltpu.SMEM((2, TPB * NB), jnp.int32),
            pltpu.VMEM((NB, M, BLK), f32),
            pltpu.VMEM((3, 2, M, OBS), f32),
            pltpu.VMEM((3, 2, OBS), f32),
            pltpu.VMEM((12, BLK, M), bf16),
            pltpu.VMEM((12, BLK, M), bf16),
            pltpu.VMEM((12, M, BLK), bf16),
            pltpu.VMEM((12, M, BLK), bf16),
            pltpu.VMEM((12, BLK, BLK), f32),
            pltpu.VMEM((12, BLK, BLK), f32),
            dma((4,)),
            dma((NB,)),
            dma((2,)),
            dma,
            dma,
            dma((2,)),
            dma,
            dma((MEM,)),
            dma((2,)),
            dma((2,)),
            dma((NB,)),
            pltpu.SemaphoreType.REGULAR((5, 2)),
        ],
        compiler_params=pltpu.CompilerParams(
            collective_id=0, has_side_effects=True, vmem_limit_bytes=48 * 1024 * 1024
        ),
        name="update",
    )(*(pinned(a) for a in (tile_list[0, 0], tile_counts, state, obs_ensemble, innovations, obs_coords)))


def solution(mesh):
    return jax.shard_map(
        shards,
        mesh=mesh,
        in_specs=(
            P("mem", "dom"),
            P("mem", "dom"),
            P("mem", "dom"),
            P(None, "dom"),
            P("dom", "mem", None, None),
            P("dom", "mem"),
        ),
        out_specs=P(None, ("dom", "mem")),
        check_vma=False,
    )
```

```python
import jax
import jax.numpy as jnp
from jax import lax
from jax.experimental import pallas as pl
from jax.experimental.pallas import tpu as pltpu
from jax.sharding import PartitionSpec as P

taper_reach = 0.6
f32, bf16 = jnp.float32, jnp.bfloat16
ZN, YN = 8, 4
MEM = ZN * YN
DOM = 8
ROWS = 32
M = 1024
OBS = 512
BLK = 128
NB = 8
TPB = 6
PTS = NB * BLK


def halves(v):
    high = v.astype(bf16)
    return high, (v - high.astype(f32)).astype(bf16)


def remote(src, dst, send, recv, device):
    return pltpu.make_async_remote_copy(
        src_ref=src,
        dst_ref=dst,
        send_sem=send,
        recv_sem=recv,
        device_id=device,
        device_id_type=pl.DeviceIdType.MESH,
    )


def kernel(
    tiles_hbm, count, state, ens, innov, coords, out,
    tiles, xbuf, win, crd, at_hi, at_lo, in_hi, in_lo, cx, cy,
    obs_local, own_local, crd_send, z_send, y_send, x_send, a_send,
    blk_recv, x_recv, crd_recv, a_recv, token,
):
    d = lax.axis_index("dom")
    me = lax.axis_index("mem")
    z, y = lax.div(me, YN), lax.rem(me, YN)
    right, left = lax.rem(d + 1, DOM), lax.rem(d + DOM - 1, DOM)

    def mem_of(dz, dy):
        return lax.rem(z + dz + ZN, ZN) * YN + lax.rem(y + dy + YN, YN)

    def rows(m):
        return pl.ds(pl.multiple_of(m * ROWS, ROWS), ROWS)

    own_obs = [
        pltpu.make_async_copy(ens, win.at[1, 0, rows(me), :], obs_local.at[0]),
        pltpu.make_async_copy(innov, win.at[1, 1, rows(me), :], obs_local.at[1]),
    ]
    small = [
        pltpu.make_async_copy(coords, crd.at[1], obs_local.at[2]),
        pltpu.make_async_copy(tiles_hbm, tiles, obs_local.at[3]),
    ]
    for c in own_obs + small:
        c.start()

    def own_state(k):
        cols = pl.ds(pl.multiple_of(me * PTS + k * BLK, BLK), BLK)
        return pltpu.make_async_copy(state.at[:, cols], xbuf.at[k, rows(me), :], own_local.at[k])

    barrier = pltpu.get_barrier_semaphore()
    around = [(d, mem_of(1, 0)), (d, mem_of(-1, 0)), (d, mem_of(0, 1)), (d, mem_of(0, -1))]

    def signal(sem, device):
        pl.semaphore_signal(sem, inc=1, device_id=device, device_id_type=pl.DeviceIdType.MESH)

    for device in around + [(left, me), (right, me)]:
        signal(barrier, device)
    for c in own_obs:
        c.wait()
    pl.semaphore_wait(barrier, 6)

    def block(m):
        return win.at[1, :, rows(m), :]

    def half(t, m):
        return win.at[1, t, rows(m), :]

    def push(src, m, dz, dy, send):
        remote(src, src, send, blk_recv.at[m], (d, mem_of(dz, dy))).start()

    def push_z(m, way):
        push(block(m), m, way, 0, z_send)

    def push_y(m):
        push(block(m), m, 0, 1, y_send)
        push(block(m), m, 0, -1, y_send)

    def push_x(m):
        remote(block(m), win.at[2, :, rows(m), :], x_send.at[0], x_recv.at[1], (left, me)).start()
        remote(block(m), win.at[0, :, rows(m), :], x_send.at[1], x_recv.at[0], (right, me)).start()

    def take(m):
        remote(block(m), block(m), z_send, blk_recv.at[m], (d, mem_of(1, 0))).wait_recv()

    def send_to(k, to):
        cols = pl.ds(pl.multiple_of(to * PTS + k * BLK, BLK), BLK)
        remote(state.at[:, cols], xbuf.at[k, rows(me), :], a_send, a_recv.at[k], (d, to)).start()

    def send(shifts, first, end):
        def one(k, c):
            for dz, dy in shifts:
                send_to(k, mem_of(dz, dy))
            return c

        lax.fori_loop(first, end, one, 0)

    def send_state(k):
        def one(i, c):
            wide, mid = i < ZN, i < 3 * ZN - 2
            j = jnp.where(wide, i, jnp.where(mid, lax.div(i - ZN, 2), i - (3 * ZN - 2)))
            dy = jnp.where(wide, 2, jnp.where(mid, 1 + 2 * lax.rem(i, 2), 0))
            h = lax.div(j + 1, 2)
            dz = jnp.where(lax.rem(j, 2) == 1, ZN // 2 - h, ZN // 2 + h)
            send_to(k, mem_of(dz, dy))
            return c

        lax.fori_loop(0, MEM - 5, one, 0)

    def column(dz):
        lo, hi = mem_of(dz, -1), mem_of(dz, 1)
        take(lo)
        push(half(0, lo), lo, 0, 1, y_send)
        push_x(lo)
        take(hi)
        push(half(1, hi), hi, 0, -1, y_send)
        push_x(hi)

    def pass_token(n, side):
        for w in range(2):
            signal(token.at[n, w], side[w])

    def await_token(n):
        for w in range(2):
            pl.semaphore_wait(token.at[n, w], 1)

    near_z, near_y = [(1, 0), (-1, 0)], [(0, 1), (0, -1)]
    pass_token(0, around[2:])
    push_z(me, 1)
    push_z(me, -1)
    send(near_z, 0, 2)
    await_token(0)
    pass_token(1, around[:2])
    push_y(me)
    send(near_z, 2, NB - 1)
    push_x(me)
    coord_copies = [
        remote(coords, crd.at[2], crd_send.at[0], crd_recv.at[1], (left, me)),
        remote(coords, crd.at[0], crd_send.at[1], crd_recv.at[0], (right, me)),
    ]
    for c in coord_copies:
        c.start()
    send(near_y, 0, NB - 1)
    await_token(1)
    for n in range(1, ZN // 2 + 1):
        if n < ZN // 2:
            pass_token(n + 1, around[:2])
        if n == 1:
            send([(dz, dy) for dz in (1, -1) for dy in (2, 1, -1)], 0, 1)
            send([(0, 2)], 0, 1)
        else:
            for dz in ([n, -n] if n < ZN // 2 else [n]):
                send([(dz, dy) for dy in (2, 1, -1, 0)], 0, 1)
        if n < ZN // 2:
            await_token(n + 1)
    for k in range(NB):
        own_state(k).start()
    for s in range(1, ZN // 2 + 1):
        if s < ZN // 2:
            up, down = mem_of(-s, 0), mem_of(s, 0)
            for m, way, t in ((up, 1, 0), (down, -1, 1)):
                take(m)
                if s < ZN // 2 - 1:
                    push_z(m, way)
                else:
                    push(half(t, m), m, way, 0, z_send)
                push_y(m)
                push_x(m)
        else:
            m = mem_of(s, 0)
            take(m)
            push_y(m)
            push_x(m)
        column(1 - s)
        if s > 1:
            column(s - 1)
        send_state(s)
    column(ZN // 2)
    send_state(5)

    def far(dz, c):
        m = mem_of(dz, 2)
        take(m)
        push_x(m)
        return c

    lax.fori_loop(0, ZN, far, 0)
    send_state(6)
    send_state(7)
    send(near_z + near_y, NB - 1, NB)

    def prepare(slot):
        def one(j, c):
            b = slot * (OBS // BLK) + j
            cols = pl.ds(pl.multiple_of(j * BLK, BLK), BLK)
            v = win[slot, 0, :, cols]
            v = v - jnp.sum(v, axis=0, keepdims=True) * (1.0 / M)
            at_hi[b], at_lo[b] = halves(v.T)
            in_hi[b], in_lo[b] = halves(win[slot, 1, :, cols])
            cx[b] = jnp.broadcast_to(crd[slot, 0:1, cols], (BLK, BLK)).T
            cy[b] = jnp.broadcast_to(crd[slot, 1:2, cols], (BLK, BLK)).T
            return c

        lax.fori_loop(0, OBS // BLK, one, 0)

    for c in small:
        c.wait()
    prepare(1)
    for c in coord_copies:
        c.wait()
    for slot, n in ((0, 0), (2, 1)):
        pltpu.make_async_copy(win.at[slot], win.at[slot], x_recv.at[n]).wait()
        prepare(slot)

    def piece(k, c):
        got = xbuf.at[k, pl.ds(0, M - ROWS), :]
        pltpu.make_async_copy(got, got, a_recv.at[k]).wait()
        own_state(k).wait()
        ids = [tiles[1, k * TPB + t] for t in range(TPB)]
        x = xbuf[k]
        xh, xl = halves(x)
        xs = jnp.concatenate([xh, xl], axis=1)
        ah = jnp.concatenate([at_hi[b] for b in ids], axis=0)
        al = jnp.concatenate([at_lo[b] for b in ids], axis=0)
        c1 = jnp.dot(ah, xs, preferred_element_type=f32)
        c2 = jnp.dot(al, xh, preferred_element_type=f32)
        cov = c1[:, :BLK] + (c1[:, BLK:] + c2)
        lane = lax.broadcasted_iota(jnp.int32, (1, BLK), 1)
        px = d.astype(f32) + (lax.rem(lane, 32).astype(f32) + 0.5) / 32.0
        first = me * (PTS // 32) + k * (BLK // 32)
        py = ((first + lax.div(lane, 32)).astype(f32) + 0.5) / float(MEM * PTS // 32)
        w = []
        for t in range(TPB):
            gx = jnp.abs(px - cx[ids[t]])
            gx = jnp.minimum(gx, float(DOM) - gx)
            gy = py - cy[ids[t]]
            taper = jnp.exp(-(gx * gx + gy * gy) / (2.0 * taper_reach * taper_reach))
            alive = jnp.where(k * TPB + t < count[0, 0], 1.0 / (M - 1), 0.0)
            w.append(taper * cov[t * BLK : (t + 1) * BLK] * alive)
        wh, wl = halves(jnp.concatenate(w, axis=0))
        ws = jnp.concatenate([wh, wl], axis=1)
        ih = jnp.concatenate([in_hi[b] for b in ids], axis=1)
        il = jnp.concatenate([in_lo[b] for b in ids], axis=1)
        r1 = jnp.dot(ih, ws, preferred_element_type=f32)
        r2 = jnp.dot(il, wh, preferred_element_type=f32)

        cols = pl.ds(pl.multiple_of(k * BLK, BLK), BLK)
        out[:, cols] = x + (r1[:, :BLK] + (r1[:, BLK:] + r2))
        return c

    lax.fori_loop(0, NB, piece, 0)

    def drain(ref, sem):
        pltpu.make_async_copy(ref, ref, sem).wait()

    drain(win.at[1, :, pl.ds(0, 7 * ROWS), :], z_send)
    drain(win.at[1, :, pl.ds(0, 24 * ROWS), :], y_send)
    drain(win.at[1], x_send.at[0])
    drain(win.at[1], x_send.at[1])
    drain(state.at[:, pl.ds(0, (MEM - 1) * PTS)], a_send)


def pinned(a):
    return a if a.size == 1 else pltpu.with_memory_space_constraint(a, pltpu.HBM)


def shards(state, obs_ensemble, innovations, obs_coords, tile_list, tile_counts):
    hbm = pl.BlockSpec(memory_space=pltpu.HBM)
    vmem = pl.BlockSpec(memory_space=pltpu.VMEM)
    dma = pltpu.SemaphoreType.DMA
    return pl.pallas_call(
        kernel,
        out_shape=pltpu.VMEM((M, PTS), f32),
        in_specs=[hbm, pl.BlockSpec(memory_space=pltpu.SMEM), hbm, hbm, hbm, hbm],
        out_specs=vmem,
        scratch_shapes=[
            pltpu.SMEM((2, TPB * NB), jnp.int32),
            pltpu.VMEM((NB, M, BLK), f32),
            pltpu.VMEM((3, 2, M, OBS), f32),
            pltpu.VMEM((3, 2, OBS), f32),
            pltpu.VMEM((12, BLK, M), bf16),
            pltpu.VMEM((12, BLK, M), bf16),
            pltpu.VMEM((12, M, BLK), bf16),
            pltpu.VMEM((12, M, BLK), bf16),
            pltpu.VMEM((12, BLK, BLK), f32),
            pltpu.VMEM((12, BLK, BLK), f32),
            dma((4,)),
            dma((NB,)),
            dma((2,)),
            dma,
            dma,
            dma((2,)),
            dma,
            dma((MEM,)),
            dma((2,)),
            dma((2,)),
            dma((NB,)),
            pltpu.SemaphoreType.REGULAR((5, 2)),
        ],
        compiler_params=pltpu.CompilerParams(
            collective_id=0, has_side_effects=True, vmem_limit_bytes=48 * 1024 * 1024
        ),
        name="update",
    )(*(pinned(a) for a in (tile_list[0, 0], tile_counts, state, obs_ensemble, innovations, obs_coords)))


def solution(mesh):
    return jax.shard_map(
        shards,
        mesh=mesh,
        in_specs=(
            P("mem", "dom"),
            P("mem", "dom"),
            P("mem", "dom"),
            P(None, "dom"),
            P("dom", "mem", None, None),
            P("dom", "mem"),
        ),
        out_specs=P(None, ("dom", "mem")),
        check_vma=False,
    )
```

```python
import jax
import jax.numpy as jnp
from jax import lax
from jax.experimental import pallas as pl
from jax.experimental.pallas import tpu as pltpu
from jax.sharding import PartitionSpec as P

taper_reach = 0.6
f32, bf16 = jnp.float32, jnp.bfloat16
ZN, YN = 8, 4
MEM = ZN * YN
DOM = 8
ROWS = 32
M = 1024
OBS = 512
BLK = 128
NB = 8
TPB = 6
PTS = NB * BLK


def halves(v):
    high = v.astype(bf16)
    return high, (v - high.astype(f32)).astype(bf16)


def weights(x, ah, al, taper):
    xh, xl = halves(x)
    xs = jnp.concatenate([xh, xl], axis=1)
    c1 = jnp.dot(ah, xs, preferred_element_type=f32)
    c2 = jnp.dot(al, xh, preferred_element_type=f32)
    wh, wl = halves(taper * (c1[:, :BLK] + (c1[:, BLK:] + c2)))
    return wh, jnp.concatenate([wh, wl], axis=1)


def moved(x, ih, il, wh, ws):
    r1 = jnp.dot(ih, ws, preferred_element_type=f32)
    r2 = jnp.dot(il, wh, preferred_element_type=f32)
    return x + (r1[:, :BLK] + (r1[:, BLK:] + r2))


def updated(x, ah, al, ih, il, taper):
    return moved(x, ih, il, *weights(x, ah, al, taper))


def finish(part, ah, al, ih, il, taper, out, piece, sem):
    done = (NB - 1) * BLK
    before = []
    for n in range(4):
        rows = pl.ds(n * (M // 4), M // 4)
        before.append(
            pltpu.make_async_copy(part.at[rows, pl.ds(0, done)], out.at[rows, pl.ds(0, done)], sem.at[n])
        )
    for c in before:
        c.start()
    wh, ws = weights(part[:, done:], ah[...], al[...], taper[...])
    after = []
    for n in range(4):
        rows = pl.ds(n * (M // 4), M // 4)
        piece[rows, :] = moved(part[rows, done:], ih[rows, :], il[rows, :], wh, ws)
        c = pltpu.make_async_copy(piece.at[rows, :], out.at[rows, pl.ds(done, BLK)], sem.at[4 + n])
        c.start()
        after.append(c)
    for c in before + after:
        c.wait()


def remote(src, dst, send, recv, device):
    return pltpu.make_async_remote_copy(
        src_ref=src,
        dst_ref=dst,
        send_sem=send,
        recv_sem=recv,
        device_id=device,
        device_id_type=pl.DeviceIdType.MESH,
    )


def kernel(
    tiles_hbm, count, state, ens, innov, coords,
    out, last_ah, last_al, last_ih, last_il, last_taper,
    tiles, xbuf, win, crd, at_hi, at_lo, in_hi, in_lo, cx, cy,
    obs_local, own_local, crd_send, z_send, y_send, x_send, a_send,
    blk_recv, x_recv, crd_recv, a_recv, token,
):
    d = lax.axis_index("dom")
    me = lax.axis_index("mem")
    z, y = lax.div(me, YN), lax.rem(me, YN)
    right, left = lax.rem(d + 1, DOM), lax.rem(d + DOM - 1, DOM)

    def mem_of(dz, dy):
        return lax.rem(z + dz + ZN, ZN) * YN + lax.rem(y + dy + YN, YN)

    def rows(m):
        return pl.ds(pl.multiple_of(m * ROWS, ROWS), ROWS)

    own_obs = [
        pltpu.make_async_copy(ens, win.at[1, 0, rows(me), :], obs_local.at[0]),
        pltpu.make_async_copy(innov, win.at[1, 1, rows(me), :], obs_local.at[1]),
    ]
    small = [
        pltpu.make_async_copy(coords, crd.at[1], obs_local.at[2]),
        pltpu.make_async_copy(tiles_hbm, tiles, obs_local.at[3]),
    ]
    for c in own_obs + small:
        c.start()

    def own_state(k):
        cols = pl.ds(pl.multiple_of(me * PTS + k * BLK, BLK), BLK)
        return pltpu.make_async_copy(state.at[:, cols], xbuf.at[k, rows(me), :], own_local.at[k])

    barrier = pltpu.get_barrier_semaphore()
    around = [(d, mem_of(1, 0)), (d, mem_of(-1, 0)), (d, mem_of(0, 1)), (d, mem_of(0, -1))]

    def signal(sem, device):
        pl.semaphore_signal(sem, inc=1, device_id=device, device_id_type=pl.DeviceIdType.MESH)

    for device in around + [(left, me), (right, me)]:
        signal(barrier, device)
    for c in own_obs:
        c.wait()
    pl.semaphore_wait(barrier, 6)

    def block(m):
        return win.at[1, :, rows(m), :]

    def half(t, m):
        return win.at[1, t, rows(m), :]

    def push(src, m, dz, dy, send):
        remote(src, src, send, blk_recv.at[m], (d, mem_of(dz, dy))).start()

    def push_z(m, way):
        push(block(m), m, way, 0, z_send)

    def push_y(m):
        push(block(m), m, 0, 1, y_send)
        push(block(m), m, 0, -1, y_send)

    def push_x(m):
        remote(block(m), win.at[2, :, rows(m), :], x_send.at[0], x_recv.at[1], (left, me)).start()
        remote(block(m), win.at[0, :, rows(m), :], x_send.at[1], x_recv.at[0], (right, me)).start()

    def take(m):
        remote(block(m), block(m), z_send, blk_recv.at[m], (d, mem_of(1, 0))).wait_recv()

    def send_to(k, to):
        cols = pl.ds(pl.multiple_of(to * PTS + k * BLK, BLK), BLK)
        remote(state.at[:, cols], xbuf.at[k, rows(me), :], a_send, a_recv.at[k], (d, to)).start()

    def send(shifts, first, end):
        def one(k, c):
            for dz, dy in shifts:
                send_to(k, mem_of(dz, dy))
            return c

        lax.fori_loop(first, end, one, 0)

    def send_state(k):
        def one(i, c):
            wide, mid = i < ZN, i < 3 * ZN - 2
            j = jnp.where(wide, i, jnp.where(mid, lax.div(i - ZN, 2), i - (3 * ZN - 2)))
            dy = jnp.where(wide, 2, jnp.where(mid, 1 + 2 * lax.rem(i, 2), 0))
            h = lax.div(j + 1, 2)
            dz = jnp.where(lax.rem(j, 2) == 1, ZN // 2 - h, ZN // 2 + h)
            send_to(k, mem_of(dz, dy))
            return c

        lax.fori_loop(0, MEM - 5, one, 0)

    def column(dz):
        lo, hi = mem_of(dz, -1), mem_of(dz, 1)
        take(lo)
        push(half(0, lo), lo, 0, 1, y_send)
        push_x(lo)
        take(hi)
        push(half(1, hi), hi, 0, -1, y_send)
        push_x(hi)

    def ring(s):
        if s < ZN // 2:
            for m, way, t in ((mem_of(-s, 0), 1, 0), (mem_of(s, 0), -1, 1)):
                take(m)
                if s < ZN // 2 - 1:
                    push_z(m, way)
                else:
                    push(half(t, m), m, way, 0, z_send)
                push_y(m)
                push_x(m)
        else:
            m = mem_of(s, 0)
            take(m)
            push_y(m)
            push_x(m)

    def pass_token(n, side):
        for w in range(2):
            signal(token.at[n, w], side[w])

    def await_token(n):
        for w in range(2):
            pl.semaphore_wait(token.at[n, w], 1)

    near_z, near_y = [(1, 0), (-1, 0)], [(0, 1), (0, -1)]
    pass_token(0, around[2:])
    push_z(me, 1)
    push_z(me, -1)
    send(near_z, 0, 2)
    await_token(0)
    pass_token(1, around[:2])
    push_y(me)
    send(near_z, 2, NB - 1)
    push_x(me)
    coord_copies = [
        remote(coords, crd.at[2], crd_send.at[0], crd_recv.at[1], (left, me)),
        remote(coords, crd.at[0], crd_send.at[1], crd_recv.at[0], (right, me)),
    ]
    for c in coord_copies:
        c.start()
    send(near_y, 0, NB - 1)
    await_token(1)
    for n in range(1, ZN // 2 + 1):
        if n < ZN // 2:
            pass_token(n + 1, around[:2])
        if n == 1:
            ring(1)
            send([(dz, dy) for dz in (1, -1) for dy in (2, 1, -1)], 0, 1)
            send([(0, 2)], 0, 1)
        else:
            for dz in ([n, -n] if n < ZN // 2 else [n]):
                send([(dz, dy) for dy in (2, 1, -1, 0)], 0, 1)
        if n < ZN // 2:
            await_token(n + 1)
    for k in range(NB):
        own_state(k).start()
    for s in range(1, ZN // 2 + 1):
        if s > 1:
            ring(s)
        column(1 - s)
        if s > 1:
            column(s - 1)
        send_state(s)
    column(ZN // 2)
    send_state(5)

    def far(dz, c):
        m = mem_of(dz, 2)
        take(m)
        push_x(m)
        return c

    lax.fori_loop(0, ZN, far, 0)
    send_state(6)
    send_state(7)
    send(near_z + near_y, NB - 1, NB)

    def prepare(slot):
        def one(j, c):
            b = slot * (OBS // BLK) + j
            cols = pl.ds(pl.multiple_of(j * BLK, BLK), BLK)
            v = win[slot, 0, :, cols]
            v = v - jnp.sum(v, axis=0, keepdims=True) * (1.0 / M)
            at_hi[b], at_lo[b] = halves(v.T)
            in_hi[b], in_lo[b] = halves(win[slot, 1, :, cols])
            cx[b] = jnp.broadcast_to(crd[slot, 0:1, cols], (BLK, BLK)).T
            cy[b] = jnp.broadcast_to(crd[slot, 1:2, cols], (BLK, BLK)).T
            return c

        lax.fori_loop(0, OBS // BLK, one, 0)

    for c in small:
        c.wait()
    prepare(1)
    for c in coord_copies:
        c.wait()
    for slot, n in ((0, 0), (2, 1)):
        pltpu.make_async_copy(win.at[slot], win.at[slot], x_recv.at[n]).wait()
        prepare(slot)

    def gather(k):
        ids = [tiles[1, k * TPB + t] for t in range(TPB)]
        lane = lax.broadcasted_iota(jnp.int32, (1, BLK), 1)
        px = d.astype(f32) + (lax.rem(lane, 32).astype(f32) + 0.5) / 32.0
        first = me * (PTS // 32) + k * (BLK // 32)
        py = ((first + lax.div(lane, 32)).astype(f32) + 0.5) / float(MEM * PTS // 32)
        w = []
        for t in range(TPB):
            gx = jnp.abs(px - cx[ids[t]])
            gx = jnp.minimum(gx, float(DOM) - gx)
            gy = py - cy[ids[t]]
            taper = jnp.exp(-(gx * gx + gy * gy) / (2.0 * taper_reach * taper_reach))
            w.append(taper * jnp.where(k * TPB + t < count[0, 0], 1.0 / (M - 1), 0.0))
        return (
            jnp.concatenate([at_hi[b] for b in ids], axis=0),
            jnp.concatenate([at_lo[b] for b in ids], axis=0),
            jnp.concatenate([in_hi[b] for b in ids], axis=1),
            jnp.concatenate([in_lo[b] for b in ids], axis=1),
            jnp.concatenate(w, axis=0),
        )

    def arrive(k):
        got = xbuf.at[k, pl.ds(0, M - ROWS), :]
        pltpu.make_async_copy(got, got, a_recv.at[k]).wait()
        own_state(k).wait()

    def piece(k, c):
        arrive(k)
        cols = pl.ds(pl.multiple_of(k * BLK, BLK), BLK)
        out[:, cols] = updated(xbuf[k], *gather(k))
        return c

    lax.fori_loop(0, NB - 1, piece, 0)
    for ref, v in zip((last_ah, last_al, last_ih, last_il, last_taper), gather(NB - 1)):
        ref[...] = v
    arrive(NB - 1)
    out[:, (NB - 1) * BLK :] = xbuf[NB - 1]

    def drain(ref, sem):
        pltpu.make_async_copy(ref, ref, sem).wait()

    drain(win.at[1, :, pl.ds(0, 7 * ROWS), :], z_send)
    drain(win.at[1, :, pl.ds(0, 24 * ROWS), :], y_send)
    drain(win.at[1], x_send.at[0])
    drain(win.at[1], x_send.at[1])
    drain(state.at[:, pl.ds(0, (MEM - 1) * PTS)], a_send)


def pinned(a):
    return a if a.size == 1 else pltpu.with_memory_space_constraint(a, pltpu.HBM)


def shards(state, obs_ensemble, innovations, obs_coords, tile_list, tile_counts):
    hbm = pl.BlockSpec(memory_space=pltpu.HBM)
    vmem = pl.BlockSpec(memory_space=pltpu.VMEM)
    dma = pltpu.SemaphoreType.DMA
    kept = (
        pltpu.VMEM((M, PTS), f32),
        pltpu.VMEM((TPB * BLK, M), bf16),
        pltpu.VMEM((TPB * BLK, M), bf16),
        pltpu.VMEM((M, TPB * BLK), bf16),
        pltpu.VMEM((M, TPB * BLK), bf16),
        pltpu.VMEM((TPB * BLK, BLK), f32),
    )
    held = pl.pallas_call(
        kernel,
        out_shape=kept,
        in_specs=[hbm, pl.BlockSpec(memory_space=pltpu.SMEM), hbm, hbm, hbm, hbm],
        out_specs=(vmem,) * 6,
        scratch_shapes=[
            pltpu.SMEM((2, TPB * NB), jnp.int32),
            pltpu.VMEM((NB, M, BLK), f32),
            pltpu.VMEM((3, 2, M, OBS), f32),
            pltpu.VMEM((3, 2, OBS), f32),
            pltpu.VMEM((12, BLK, M), bf16),
            pltpu.VMEM((12, BLK, M), bf16),
            pltpu.VMEM((12, M, BLK), bf16),
            pltpu.VMEM((12, M, BLK), bf16),
            pltpu.VMEM((12, BLK, BLK), f32),
            pltpu.VMEM((12, BLK, BLK), f32),
            dma((4,)),
            dma((NB,)),
            dma((2,)),
            dma,
            dma,
            dma((2,)),
            dma,
            dma((MEM,)),
            dma((2,)),
            dma((2,)),
            dma((NB,)),
            pltpu.SemaphoreType.REGULAR((5, 2)),
        ],
        compiler_params=pltpu.CompilerParams(
            collective_id=0, has_side_effects=True, vmem_limit_bytes=46 * 1024 * 1024
        ),
        name="update",
    )(*(pinned(a) for a in (tile_list[0, 0], tile_counts, state, obs_ensemble, innovations, obs_coords)))
    return pl.pallas_call(
        finish,
        out_shape=jax.ShapeDtypeStruct((M, PTS), f32),
        in_specs=[vmem] * 6,
        out_specs=pl.BlockSpec(memory_space=pl.ANY),
        scratch_shapes=[pltpu.VMEM((M, BLK), f32), dma((8,))],
        compiler_params=pltpu.CompilerParams(vmem_limit_bytes=16 * 1024 * 1024),
        name="finish",
    )(*(pltpu.with_memory_space_constraint(a, pltpu.VMEM) for a in held))


def solution(mesh):
    return jax.shard_map(
        shards,
        mesh=mesh,
        in_specs=(
            P("mem", "dom"),
            P("mem", "dom"),
            P("mem", "dom"),
            P(None, "dom"),
            P("dom", "mem", None, None),
            P("dom", "mem"),
        ),
        out_specs=P(None, ("dom", "mem")),
        check_vma=False,
    )
```
